32 devices in a mesh: val: 2 (over x), pts: 16 (over z, y, core).
Axes of the slice: x: 2, y: 2, z: 4, core: 2. Of those that a mesh axis runs over, the one named last changes fastest.
Arguments:
- trial: bfloat16 [512, 16384], P('val', 'pts'), may hold values from -6 to 6
- energy_gap: float32 [512, 512], P('val', 'pts'), may hold values from 0.5 to 3.5
- orb_val: bfloat16 [512, 16384], P('val'), may hold values from -0.25 to 0.25
- orb_cond: bfloat16 [512, 16384], P('pts'), may hold values from -0.25 to 0.25
- kernel: bfloat16 [16384, 16384], P('pts', 'val'), may hold values from -0.046875 to 0.046875
Outputs:
- first_step: bfloat16 [512, 16384], P('val', 'pts')
- filtered: bfloat16 [512, 16384], P('val', 'pts')
The draws below stay inside these ranges and needn't reach their ends.
All inputs are finite; a program needn't handle non-finite values.
Results may differ from the reference program's by a relative error of at most 0.029.
Values may be sent and summed in bfloat16 or wider, within the bound.
A program may use at most 128 MiB of HBM per device.

```python
import math
import jax
import jax.numpy as jnp
from jax import lax

NV = 512
NC = 512
NMU = 16384
K = 32


def block_scale(stream_key, extent, shards, low, largest):
    gain, own = 1.0, jax.random.fold_in(stream_key, 6)
    for position, shards_of in shards:
        draws = jnp.exp(jax.random.uniform(jax.random.fold_in(own, position), (shards_of,), jnp.float32, low / len(shards), largest / len(shards)))
        gain = gain * jnp.repeat(draws, extent[position] // shards_of).reshape([-1 if axis == position else 1 for axis in range(len(extent))])
    return gain


def bell_draw(rng, shape, width, bound, split=(), held_as=jnp.bfloat16):
    gain = block_scale(rng, shape, split, -0.22, 0.18) if split else 1.0
    drawn = jax.random.normal(rng, shape, jnp.float32) * width * gain
    return jnp.minimum(jnp.maximum(drawn, -bound), bound).astype(held_as)


def setup_inputs(seed: int = 0) -> dict:
    key_of = jax.random.split(jax.random.key(seed), 6)
    trial = bell_draw(key_of[0], (NV, NC * K), 1.0, 6.0, ((0, 2), (1, 16)))
    energy_gap = jnp.clip(0.5 + 3.0 * jax.random.uniform(key_of[1], (NV, NC), jnp.float32) ** block_scale(key_of[1], (NV, NC), ((0, 2), (1, 16)), -0.2, 0.2), 0.5, 3.5)
    orb_val = bell_draw(key_of[2], (NV, NMU), NV ** -0.5, 0.25, ((0, 2),))
    orb_cond = bell_draw(key_of[3], (NC, NMU), NC ** -0.5, 0.25, ((0, 16),))
    kernel = bell_draw(key_of[4], (NMU, NMU), NMU ** -0.5, 0.046875, ((0, 16), (1, 2)))
    return dict(trial=trial, energy_gap=energy_gap, orb_val=orb_val, orb_cond=orb_cond, kernel=kernel)


CENTER = 2.0
HALF_WIDTH = 1.5


def pair_table(val_cols, cond_cols):
    table = val_cols.astype(jnp.float32)[:, None, :] * cond_cols.astype(jnp.float32)[None, :, :]
    return table.reshape(val_cols.shape[0] * cond_cols.shape[0], val_cols.shape[1]).astype(jnp.bfloat16)


def coupling(trial_flat, orb_val, orb_cond, kernel):
    trial_rows = trial_flat.reshape(NV * NC, K)
    block_len = math.gcd(NMU, 512)
    block_count = NMU // block_len

    def block_pairs(number):
        offset = (number * block_len).astype(jnp.int32)
        return offset, pair_table(lax.dynamic_slice_in_dim(orb_val, offset, block_len, 1),
                                  lax.dynamic_slice_in_dim(orb_cond, offset, block_len, 1))

    def encode_block(number):
        offset, pairs = block_pairs(number)
        return lax.dot_general(trial_rows, pairs, (((0,), (0,)), ((), ())), preferred_element_type=jnp.float32)

    encoded = lax.map(encode_block, jnp.arange(block_count, dtype=jnp.int32))
    fit_coefs = jnp.transpose(encoded, (1, 0, 2)).reshape(K, NMU).astype(jnp.bfloat16)
    kernel_out = lax.dot_general(fit_coefs, kernel, (((1,), (1,)), ((), ())),
                                 preferred_element_type=jnp.float32).astype(jnp.bfloat16)

    def decode_block(total_sum, number):
        offset, pairs = block_pairs(number)
        coef_block = lax.dynamic_slice_in_dim(kernel_out, offset, block_len, 1)
        added = lax.dot_general(pairs, coef_block, (((1,), (1,)), ((), ())), preferred_element_type=jnp.float32)
        return total_sum + added, None

    decoded, unused = lax.scan(decode_block, jnp.zeros((NV * NC, K), jnp.float32),
                               jnp.arange(block_count, dtype=jnp.int32))
    return decoded.reshape(NV, NC, K)


def filter_apply(trial_flat, energy_gap, orb_val, orb_cond, kernel):
    current = trial_flat.astype(jnp.float32).reshape(NV, NC, K)
    coupled = coupling(trial_flat, orb_val, orb_cond, kernel)
    return (energy_gap[:, :, None] * current + 2.0 * coupled - CENTER * current) / HALF_WIDTH


def reference(trial, energy_gap, orb_val, orb_cond, kernel):
    first_step = filter_apply(trial, energy_gap, orb_val, orb_cond, kernel).reshape(NV, NC * K).astype(jnp.bfloat16)
    second = 2.0 * filter_apply(first_step, energy_gap, orb_val, orb_cond, kernel)
    second = second - trial.astype(jnp.float32).reshape(NV, NC, K)
    return first_step, second.reshape(NV, NC * K).astype(jnp.bfloat16)
```

```python
import math

import jax
import jax.numpy as jnp
from jax import lax
from jax.experimental import pallas as pl
from jax.experimental.pallas import tpu as pltpu
from jax.sharding import PartitionSpec as P

CENTER = 2.0
HALF_WIDTH = 1.5


def encode_kernel(rows_ref, val_ref, cond_ref, fit_ref):
    cond_count = cond_ref.shape[0]
    k = fit_ref.shape[0]
    total = jnp.zeros(fit_ref.shape, jnp.float32)
    half = jnp.dot(rows_ref[...], val_ref[...], preferred_element_type=jnp.float32)
    for c in range(cond_count):
        total += half[c * k:(c + 1) * k, :] * cond_ref[c:c + 1, :].astype(jnp.float32)
    fit_ref[...] = total.astype(fit_ref.dtype)


def encode(rows, orb_val, orb_cond, k):
    points = orb_val.shape[1]
    width = math.gcd(points, 512)
    return pl.pallas_call(
        encode_kernel,
        out_shape=jax.ShapeDtypeStruct((k, points), jnp.bfloat16),
        grid=(points // width,),
        in_specs=[
            pl.BlockSpec(rows.shape, lambda i: (0, 0)),
            pl.BlockSpec((orb_val.shape[0], width), lambda i: (0, i)),
            pl.BlockSpec((orb_cond.shape[0], width), lambda i: (0, i)),
        ],
        out_specs=pl.BlockSpec((k, width), lambda i: (0, i)),
        name="encode",
    )(rows, orb_val, orb_cond)


def decode_kernel(val_ref, cond_ref, field_ref, out_ref):
    @pl.when(pl.program_id(0) == 0)
    def _():
        out_ref[...] = jnp.zeros_like(out_ref)

    field = field_ref[...]
    spread = jnp.concatenate(
        [field * cond_ref[c:c + 1, :] for c in range(cond_ref.shape[0])], axis=0
    )
    out_ref[...] += lax.dot_general(
        spread, val_ref[...], (((1,), (1,)), ((), ())), preferred_element_type=jnp.float32
    )


def decode(orb_val, orb_cond, field):
    k, points = field.shape
    width = math.gcd(points, 1024)
    rows = orb_cond.shape[0] * k
    return pl.pallas_call(
        decode_kernel,
        out_shape=jax.ShapeDtypeStruct((rows, orb_val.shape[0]), jnp.float32),
        grid=(points // width,),
        in_specs=[
            pl.BlockSpec((orb_val.shape[0], width), lambda i: (0, i)),
            pl.BlockSpec((orb_cond.shape[0], width), lambda i: (0, i)),
            pl.BlockSpec((k, width), lambda i: (0, i)),
        ],
        out_specs=pl.BlockSpec((rows, orb_val.shape[0]), lambda i: (0, 0)),
        name="decode",
    )(orb_val, orb_cond, field)


def filter_apply(rows, gap_rows, orb_val, orb_cond, kernel, k):
    part = encode(rows, orb_val, orb_cond, k)
    own = lax.psum_scatter(part, "val", scatter_dimension=1, tiled=True)
    fit = lax.psum(own, "pts")
    kernel_part = lax.dot_general(
        fit, kernel, (((1,), (1,)), ((), ())), preferred_element_type=jnp.float32
    )
    piece = lax.psum(kernel_part.astype(jnp.bfloat16), "val")
    field = lax.all_gather(piece, "pts", axis=1, tiled=True)
    coupled = decode(orb_val, orb_cond, field)
    current = rows.astype(jnp.float32)
    return (gap_rows * current + 2.0 * coupled - CENTER * current) / HALF_WIDTH


def on_device(trial, energy_gap, orb_val, orb_cond, kernel):
    k = trial.shape[1] // orb_cond.shape[0]
    rows = trial.T
    gap_rows = jnp.repeat(energy_gap.T, k, axis=0)
    first = filter_apply(rows, gap_rows, orb_val, orb_cond, kernel, k).astype(jnp.bfloat16)
    second = 2.0 * filter_apply(first, gap_rows, orb_val, orb_cond, kernel, k)
    second = (second - rows.astype(jnp.float32)).astype(jnp.bfloat16)
    return first.T, second.T


def solution(mesh):
    placed = (P("val", "pts"), P("val", "pts"), P("val", None), P("pts", None), P("pts", "val"))
    return jax.shard_map(
        on_device,
        mesh=mesh,
        in_specs=placed,
        out_specs=(P("val", "pts"), P("val", "pts")),
        check_vma=False,
    )
```

```python
import functools
import math

import jax
import jax.numpy as jnp
from jax import lax
from jax.experimental import pallas as pl
from jax.experimental.pallas import tpu as pltpu
from jax.sharding import PartitionSpec as P

CENTER = 2.0
HALF_WIDTH = 1.5
MESH = pl.DeviceIdType.MESH
F32 = jnp.float32
BF16 = jnp.bfloat16


def filter_kernel(sizes, rows_ref, gap_ref, cond_ref, val_hbm, kern_hbm, first_ref, second_ref,
                  val_ref, kern_ref, source, total, product, away, home, got_core, mixed, got_val, mid,
                  got_y, low, got_z, fit, part, got_part, field,
                  val_sem, kern_sem, send_sem, recv_sem):
    A, Y, Z = sizes
    Q = Y * Z
    B = 2 * Q
    k, w = fit.shape[-2:]
    R = field.shape[-1]
    cond_count = cond_ref.shape[0]
    a = lax.axis_index("val")
    p = lax.axis_index("pts")
    h = lax.rem(p, 2)
    y = lax.rem(p // 2, Y)
    z = p // (2 * Y)

    def around(base, shift, size):
        return lax.rem(base + shift + size, size)

    def at(val, zz, yy, hh):
        return (val, (zz * Y + yy) * 2 + hh)

    other = at(a, z, y, 1 - h)
    vals = [at(around(a, d, A), z, y, h) for d in range(1, A)]
    ys = [at(a, z, around(y, d, Y), h) for d in range(1, Y)]
    zs = [at(a, around(z, d, Z), y, h) for d in range(1, Z)]

    def val_copy(i):
        cols = pl.ds(pl.multiple_of(i * w, w), w)
        return pltpu.make_async_copy(val_hbm.at[:, cols], val_ref.at[:, cols], val_sem.at[i])

    def piece_number(val, half, j):
        return (val * 2 + half) * Q + j

    def fetch(val, half):
        @pl.loop(0, Q)
        def _(j):
            val_copy(piece_number(val, half, j)).start()

    order = [around(a, d, A) for d in range(1, A)] + [a]
    for half in (1 - h, h):
        for b in order:
            fetch(b, half)
    kern_copy = pltpu.make_async_copy(kern_hbm, kern_ref, kern_sem)
    kern_copy.start()

    barrier = pltpu.get_barrier_semaphore()
    peers = [other] + vals + ys + zs
    for peer in peers:
        pl.semaphore_signal(barrier, inc=1, device_id=peer, device_id_type=MESH)
    pl.semaphore_wait(barrier, len(peers))

    source[...] = rows_ref[...]

    @pl.loop(0, 2)
    def _(step):
        number = [0]
        started = []

        def send(src, dst, peer):
            slot = number[0]
            number[0] += 1
            copy = pltpu.make_async_remote_copy(
                src_ref=src, dst_ref=dst, send_sem=send_sem.at[step, slot],
                recv_sem=recv_sem.at[step, slot], device_id=peer, device_id_type=MESH)
            copy.start()
            started.append(copy)
            return copy

        def encode(val, half, target, slot):
            @pl.loop(0, Q)
            def _(j):
                i = piece_number(val, half, j)

                @pl.when(step == 0)
                def _():
                    val_copy(i).wait()

                cols = pl.ds(pl.multiple_of(i * w, w), w)
                full = jnp.dot(source[...], val_ref[:, cols], preferred_element_type=F32)
                cond = cond_ref[:, cols].astype(F32)
                summed = jnp.zeros((k, w), F32)
                for c in range(cond_count):
                    summed += full[c * k:(c + 1) * k, :] * cond[c:c + 1, :]
                target[slot, j] = summed.astype(BF16)

        core_copies = []
        for n, b in enumerate(order):
            encode(b, 1 - h, away.at[step], n)
            core_copies.append(send(away.at[step, n], got_core.at[step, n], other))
        val_copies = []
        for n, b in enumerate(order):
            encode(b, h, home.at[step], n)
            core_copies[n].wait_recv()
            mixed[step, n] = (home[step, n].astype(F32) + got_core[step, n].astype(F32)).astype(BF16)
            if n < A - 1:
                val_copies.append(send(mixed.at[step, n], got_val.at[step, n], vals[n]))
        summed = mixed[step, A - 1].astype(F32)
        for n, copy in enumerate(val_copies):
            copy.wait_recv()
            summed += got_val[step, n].astype(F32)
        mid[step] = summed.astype(BF16).reshape(mid.shape[1:])
        copies = [send(mid.at[step, around(y, n + 1, Y)], got_y.at[step, n], peer)
                  for n, peer in enumerate(ys)]
        summed = mid[step, y].astype(F32)
        for n, copy in enumerate(copies):
            copy.wait_recv()
            summed += got_y[step, n].astype(F32)
        low[step] = summed.astype(BF16)
        copies = [send(low.at[step, around(z, n + 1, Z)], got_z.at[step, n], peer)
                  for n, peer in enumerate(zs)]
        summed = low[step, z].astype(F32)
        for n, copy in enumerate(copies):
            copy.wait_recv()
            summed += got_z[step, n].astype(F32)
        fit[step, h, y, z] = summed.astype(BF16)

        def gather(buffer, use):
            mine = buffer.at[step, h, y, z]
            z_copies = [send(mine, mine, peer) for peer in zs]
            y_copies = {}
            core_copies = []

            def spread(dz):
                zz = around(z, -dz, Z)
                ref = buffer.at[step, h, y, zz]
                for n, peer in enumerate(ys):
                    y_copies[(n, dz)] = send(ref, ref, peer)
                core_copies.append((send(ref, ref, other), y, zz))
                use(h, y, zz)

            spread(0)
            for dz in range(1, Z):
                z_copies[dz - 1].wait_recv()
                spread(dz)
            for n in range(Y - 1):
                yy = around(y, -(n + 1), Y)
                for dz in range(Z):
                    zz = around(z, -dz, Z)
                    y_copies[(n, dz)].wait_recv()
                    ref = buffer.at[step, h, yy, zz]
                    core_copies.append((send(ref, ref, other), yy, zz))
                    use(h, yy, zz)
            for copy, yy, zz in core_copies:
                copy.wait_recv()
                use(1 - h, yy, zz)

        product[...] = jnp.zeros_like(product)

        @pl.when(step == 0)
        def _():
            kern_copy.wait()

        def apply_kernel(hh, yy, zz):
            cols = pl.ds(pl.multiple_of(((hh * Y + yy) * Z + zz) * w, w), w)
            product[...] += lax.dot_general(
                kern_ref[:, cols], fit[step, hh, yy, zz], (((1,), (1,)), ((), ())),
                preferred_element_type=F32)

        gather(fit, apply_kernel)
        part[step] = product[...].T.astype(BF16)
        copies = [send(part.at[step], got_part.at[step, n], peer) for n, peer in enumerate(vals)]
        summed = part[step].astype(F32)
        for n, copy in enumerate(copies):
            copy.wait_recv()
            summed += got_part[step, n].astype(F32)
        field[step, h, y, z] = summed.astype(BF16)

        total[...] = jnp.zeros_like(total)

        def decode(hh, yy, zz):
            cols = pl.ds(pl.multiple_of(((zz * Y + yy) * 2 + hh) * R, R), R)
            piece = field[step, hh, yy, zz]
            cond = cond_ref[:, cols]
            table = jnp.concatenate([piece * cond[c:c + 1, :] for c in range(cond_count)], axis=0)
            total[...] += lax.dot_general(
                table, val_ref[:, cols], (((1,), (1,)), ((), ())), preferred_element_type=F32)

        gather(field, decode)
        current = source[...].astype(F32)
        applied = (gap_ref[...] * current + 2.0 * total[...] - CENTER * current) / HALF_WIDTH

        @pl.when(step == 0)
        def _():
            source[...] = applied.astype(BF16)
            first_ref[...] = applied.astype(BF16)

        @pl.when(step == 1)
        def _():
            second_ref[...] = (2.0 * applied - rows_ref[...].astype(F32)).astype(BF16)
        for copy in started:
            copy.wait_send()


def encode_kernel(rows_ref, val_ref, cond_ref, fit_ref):
    cond_count = cond_ref.shape[0]
    k = fit_ref.shape[0]
    total = jnp.zeros(fit_ref.shape, jnp.float32)
    half = jnp.dot(rows_ref[...], val_ref[...], preferred_element_type=jnp.float32)
    for c in range(cond_count):
        total += half[c * k:(c + 1) * k, :] * cond_ref[c:c + 1, :].astype(jnp.float32)
    fit_ref[...] = total.astype(fit_ref.dtype)


def encode(rows, orb_val, orb_cond, k):
    points = orb_val.shape[1]
    width = math.gcd(points, 512)
    return pl.pallas_call(
        encode_kernel,
        out_shape=jax.ShapeDtypeStruct((k, points), jnp.bfloat16),
        grid=(points // width,),
        in_specs=[
            pl.BlockSpec(rows.shape, lambda i: (0, 0)),
            pl.BlockSpec((orb_val.shape[0], width), lambda i: (0, i)),
            pl.BlockSpec((orb_cond.shape[0], width), lambda i: (0, i)),
        ],
        out_specs=pl.BlockSpec((k, width), lambda i: (0, i)),
        name="encode",
    )(rows, orb_val, orb_cond)


def decode_kernel(val_ref, cond_ref, field_ref, out_ref):
    @pl.when(pl.program_id(0) == 0)
    def _():
        out_ref[...] = jnp.zeros_like(out_ref)

    field = field_ref[...]
    spread = jnp.concatenate(
        [field * cond_ref[c:c + 1, :] for c in range(cond_ref.shape[0])], axis=0
    )
    out_ref[...] += lax.dot_general(
        spread, val_ref[...], (((1,), (1,)), ((), ())), preferred_element_type=jnp.float32
    )


def decode(orb_val, orb_cond, field):
    k, points = field.shape
    width = math.gcd(points, 1024)
    rows = orb_cond.shape[0] * k
    return pl.pallas_call(
        decode_kernel,
        out_shape=jax.ShapeDtypeStruct((rows, orb_val.shape[0]), jnp.float32),
        grid=(points // width,),
        in_specs=[
            pl.BlockSpec((orb_val.shape[0], width), lambda i: (0, i)),
            pl.BlockSpec((orb_cond.shape[0], width), lambda i: (0, i)),
            pl.BlockSpec((k, width), lambda i: (0, i)),
        ],
        out_specs=pl.BlockSpec((rows, orb_val.shape[0]), lambda i: (0, 0)),
        name="decode",
    )(orb_val, orb_cond, field)


def staged_apply(rows, gap_rows, orb_val, orb_cond, kernel, k):
    part = encode(rows, orb_val, orb_cond, k)
    own = lax.psum_scatter(part, "val", scatter_dimension=1, tiled=True)
    fit = lax.psum(own, "pts")
    kernel_part = lax.dot_general(
        fit, kernel, (((1,), (1,)), ((), ())), preferred_element_type=jnp.float32
    )
    piece = lax.psum(kernel_part.astype(jnp.bfloat16), "val")
    field = lax.all_gather(piece, "pts", axis=1, tiled=True)
    coupled = decode(orb_val, orb_cond, field)
    current = rows.astype(jnp.float32)
    return (gap_rows * current + 2.0 * coupled - CENTER * current) / HALF_WIDTH


def on_device(A, B, trial, energy_gap, orb_val, orb_cond, kernel):
    k = trial.shape[1] // orb_cond.shape[0]
    rows = trial.T
    gap_rows = jnp.repeat(energy_gap.T, k, axis=0)
    Q = B // 2
    Z = math.gcd(Q, 4)
    Y = Q // Z
    points = orb_val.shape[1]
    w = points // (A * B)
    R = points // B
    if w % 128:
        first = staged_apply(rows, gap_rows, orb_val, orb_cond, kernel, k).astype(BF16)
        second = 2.0 * staged_apply(first, gap_rows, orb_val, orb_cond, kernel, k)
        return first.T, (second - rows.astype(F32)).astype(BF16).T
    sends = A + (A - 1) * 2 + (Y - 1) + (Z - 1) + 2 * (Z - 1 + (Y - 1) * Z + Q)
    vmem = pl.BlockSpec(memory_space=pltpu.VMEM)
    anywhere = pl.BlockSpec(memory_space=pl.ANY)
    shape = jax.ShapeDtypeStruct(rows.shape, BF16)
    first, second = pl.pallas_call(
        functools.partial(filter_kernel, (A, Y, Z)),
        out_shape=(shape, shape),
        in_specs=[vmem, vmem, vmem, anywhere, anywhere],
        out_specs=(vmem, vmem),
        scratch_shapes=[
            pltpu.VMEM(orb_val.shape, BF16),
            pltpu.VMEM(kernel.shape, BF16),
            pltpu.VMEM(rows.shape, BF16),
            pltpu.VMEM(rows.shape, F32),
            pltpu.VMEM((R, k), F32),
            pltpu.VMEM((2, A, Q, k, w), BF16),
            pltpu.VMEM((2, A, Q, k, w), BF16),
            pltpu.VMEM((2, A, Q, k, w), BF16),
            pltpu.VMEM((2, A, Q, k, w), BF16),
            pltpu.VMEM((2, max(A - 1, 1), Q, k, w), BF16),
            pltpu.VMEM((2, Y, Z, k, w), BF16),
            pltpu.VMEM((2, max(Y - 1, 1), Z, k, w), BF16),
            pltpu.VMEM((2, Z, k, w), BF16),
            pltpu.VMEM((2, max(Z - 1, 1), k, w), BF16),
            pltpu.VMEM((2, 2, Y, Z, k, w), BF16),
            pltpu.VMEM((2, k, R), BF16),
            pltpu.VMEM((2, max(A - 1, 1), k, R), BF16),
            pltpu.VMEM((2, 2, Y, Z, k, R), BF16),
            pltpu.SemaphoreType.DMA((A * B,)),
            pltpu.SemaphoreType.DMA,
            pltpu.SemaphoreType.DMA((2, sends)),
            pltpu.SemaphoreType.DMA((2, sends)),
        ],
        compiler_params=pltpu.CompilerParams(
            collective_id=0, has_side_effects=True, vmem_limit_bytes=60 << 20),
        name="filter",
    )(rows, gap_rows, orb_cond, orb_val, kernel)
    return first.T, second.T


def solution(mesh):
    placed = (P("val", "pts"), P("val", "pts"), P("val", None), P("pts", None), P("pts", "val"))
    return jax.shard_map(
        functools.partial(on_device, mesh.shape["val"], mesh.shape["pts"]),
        mesh=mesh,
        in_specs=placed,
        out_specs=(P("val", "pts"), P("val", "pts")),
        check_vma=False,
    )
```

```python
import functools
import math

import jax
import jax.numpy as jnp
from jax import lax
from jax.experimental import pallas as pl
from jax.experimental.pallas import tpu as pltpu
from jax.sharding import PartitionSpec as P

CENTER = 2.0
HALF_WIDTH = 1.5
MESH = pl.DeviceIdType.MESH
F32 = jnp.float32
BF16 = jnp.bfloat16


def filter_kernel(sizes, rows_ref, gap_ref, cond_ref, val_hbm, kern_hbm, first_ref, second_ref,
                  val_ref, kern_ref, source, total, product, away, home, got_core, mixed, got_val, mid,
                  got_y, low, got_z, fit, part, got_part, field,
                  val_sem, kern_sem, send_sem, recv_sem):
    A, Y, Z = sizes
    Q = Y * Z
    B = 2 * Q
    k, w = fit.shape[-2:]
    R = field.shape[-1]
    cond_count = cond_ref.shape[0]
    a = lax.axis_index("val")
    p = lax.axis_index("pts")
    h = lax.rem(p, 2)
    y = lax.rem(p // 2, Y)
    z = p // (2 * Y)

    def around(base, shift, size):
        return lax.rem(base + shift + size, size)

    def at(val, zz, yy, hh):
        return (val, (zz * Y + yy) * 2 + hh)

    other = at(a, z, y, 1 - h)
    vals = [at(around(a, d, A), z, y, h) for d in range(1, A)]
    ys = [at(a, z, around(y, d, Y), h) for d in range(1, Y)]
    zs = [at(a, around(z, d, Z), y, h) for d in range(1, Z)]

    def val_copy(i):
        cols = pl.ds(pl.multiple_of(i * w, w), w)
        return pltpu.make_async_copy(val_hbm.at[:, cols], val_ref.at[:, cols], val_sem.at[i])

    def piece_number(val, half, j):
        return (val * 2 + half) * Q + j

    def fetch(val, half):
        @pl.loop(0, Q)
        def _(j):
            val_copy(piece_number(val, half, j)).start()

    order = [around(a, d, A) for d in range(1, A)] + [a]
    for half in (1 - h, h):
        for b in order:
            fetch(b, half)
    kern_copy = pltpu.make_async_copy(kern_hbm, kern_ref, kern_sem)
    kern_copy.start()

    barrier = pltpu.get_barrier_semaphore()
    peers = [other] + vals + ys + zs
    for peer in peers:
        pl.semaphore_signal(barrier, inc=1, device_id=peer, device_id_type=MESH)
    pl.semaphore_wait(barrier, len(peers))

    source[...] = rows_ref[...]

    def chain(step, i):
        number = [0]
        started = []
        rows = pl.ds(i * cond_count * k, cond_count * k)

        def send(src, dst, peer):
            slot = number[0]
            number[0] += 1
            copy = pltpu.make_async_remote_copy(
                src_ref=src, dst_ref=dst, send_sem=send_sem.at[step, i, slot],
                recv_sem=recv_sem.at[step, i, slot], device_id=peer, device_id_type=MESH)
            copy.start()
            started.append(copy)
            return copy

        def encode(val, half, target, slot):
            @pl.loop(0, Q)
            def _(j):
                n = piece_number(val, half, j)
                if i == 0:
                    @pl.when(step == 0)
                    def _():
                        val_copy(n).wait()

                cols = pl.ds(pl.multiple_of(n * w, w), w)
                full = jnp.dot(source[rows, :], val_ref[:, cols], preferred_element_type=F32)
                cond = cond_ref[:, cols].astype(F32)
                summed = jnp.zeros((k, w), F32)
                for c in range(cond_count):
                    summed += full[c * k:(c + 1) * k, :] * cond[c:c + 1, :]
                target[slot, j] = summed.astype(BF16)

        core_copies = []
        for n, b in enumerate(order):
            encode(b, 1 - h, away.at[step, i], n)
            core_copies.append(send(away.at[step, i, n], got_core.at[step, i, n], other))
            yield
        val_copies = []
        for n, b in enumerate(order):
            encode(b, h, home.at[step, i], n)
            core_copies[n].wait_recv()
            mixed[step, i, n] = (home[step, i, n].astype(F32)
                                 + got_core[step, i, n].astype(F32)).astype(BF16)
            if n < A - 1:
                val_copies.append(send(mixed.at[step, i, n], got_val.at[step, i, n], vals[n]))
            yield
        summed = mixed[step, i, A - 1].astype(F32)
        for n, copy in enumerate(val_copies):
            copy.wait_recv()
            summed += got_val[step, i, n].astype(F32)
        mid[step, i] = summed.astype(BF16).reshape(mid.shape[2:])
        copies = [send(mid.at[step, i, around(y, n + 1, Y)], got_y.at[step, i, n], peer)
                  for n, peer in enumerate(ys)]
        yield
        summed = mid[step, i, y].astype(F32)
        for n, copy in enumerate(copies):
            copy.wait_recv()
            summed += got_y[step, i, n].astype(F32)
        low[step, i] = summed.astype(BF16)
        copies = [send(low.at[step, i, around(z, n + 1, Z)], got_z.at[step, i, n], peer)
                  for n, peer in enumerate(zs)]
        yield
        summed = low[step, i, z].astype(F32)
        for n, copy in enumerate(copies):
            copy.wait_recv()
            summed += got_z[step, i, n].astype(F32)
        fit[step, i, h, y, z] = summed.astype(BF16)

        def gather(buffer, use):
            mine = buffer.at[step, i, h, y, z]
            z_copies = [send(mine, mine, peer) for peer in zs]
            y_copies = {}
            core_copies = []

            def spread(dz):
                zz = around(z, -dz, Z)
                ref = buffer.at[step, i, h, y, zz]
                for n, peer in enumerate(ys):
                    y_copies[(n, dz)] = send(ref, ref, peer)
                core_copies.append((send(ref, ref, other), y, zz))
                use(h, y, zz)

            spread(0)
            yield
            for dz in range(1, Z):
                z_copies[dz - 1].wait_recv()
                spread(dz)
                yield
            for n in range(Y - 1):
                yy = around(y, -(n + 1), Y)
                for dz in range(Z):
                    zz = around(z, -dz, Z)
                    y_copies[(n, dz)].wait_recv()
                    ref = buffer.at[step, i, h, yy, zz]
                    core_copies.append((send(ref, ref, other), yy, zz))
                    use(h, yy, zz)
                    if dz % 2:
                        yield
            for n, (copy, yy, zz) in enumerate(core_copies):
                copy.wait_recv()
                use(1 - h, yy, zz)
                if n % 2:
                    yield

        product[i] = jnp.zeros(product.shape[1:], F32)
        if i == 0:
            @pl.when(step == 0)
            def _():
                kern_copy.wait()

        def apply_kernel(hh, yy, zz):
            cols = pl.ds(pl.multiple_of(((hh * Y + yy) * Z + zz) * w, w), w)
            product[i] += lax.dot_general(
                kern_ref[:, cols], fit[step, i, hh, yy, zz], (((1,), (1,)), ((), ())),
                preferred_element_type=F32)

        yield from gather(fit, apply_kernel)
        part[step, i] = product[i].T.astype(BF16)
        copies = [send(part.at[step, i], got_part.at[step, i, n], peer)
                  for n, peer in enumerate(vals)]
        yield
        summed = part[step, i].astype(F32)
        for n, copy in enumerate(copies):
            copy.wait_recv()
            summed += got_part[step, i, n].astype(F32)
        field[step, i, h, y, z] = summed.astype(BF16)

        total[rows, :] = jnp.zeros((cond_count * k, total.shape[1]), F32)

        def decode(hh, yy, zz):
            cols = pl.ds(pl.multiple_of(((zz * Y + yy) * 2 + hh) * R, R), R)
            piece = field[step, i, hh, yy, zz]
            cond = cond_ref[:, cols]
            table = jnp.concatenate([piece * cond[c:c + 1, :] for c in range(cond_count)], axis=0)
            total[rows, :] += lax.dot_general(
                table, val_ref[:, cols], (((1,), (1,)), ((), ())), preferred_element_type=F32)

        yield from gather(field, decode)
        current = source[rows, :].astype(F32)
        applied = (gap_ref[...] * current + 2.0 * total[rows, :] - CENTER * current) / HALF_WIDTH

        @pl.when(step == 0)
        def _():
            source[rows, :] = applied.astype(BF16)
            first_ref[rows, :] = applied.astype(BF16)

        @pl.when(step == 1)
        def _():
            second_ref[rows, :] = (2.0 * applied - rows_ref[rows, :].astype(F32)).astype(BF16)

        for copy in started:
            copy.wait_send()

    @pl.loop(0, 2)
    def _(step):
        live = [chain(step, 0), chain(step, 1)]
        for _ in range(2 * A - 1):
            next(live[0])
        while live:
            live = [part_chain for part_chain in live if next(part_chain, True) is None]


def encode_kernel(rows_ref, val_ref, cond_ref, fit_ref):
    cond_count = cond_ref.shape[0]
    k = fit_ref.shape[0]
    total = jnp.zeros(fit_ref.shape, jnp.float32)
    half = jnp.dot(rows_ref[...], val_ref[...], preferred_element_type=jnp.float32)
    for c in range(cond_count):
        total += half[c * k:(c + 1) * k, :] * cond_ref[c:c + 1, :].astype(jnp.float32)
    fit_ref[...] = total.astype(fit_ref.dtype)


def encode(rows, orb_val, orb_cond, k):
    points = orb_val.shape[1]
    width = math.gcd(points, 512)
    return pl.pallas_call(
        encode_kernel,
        out_shape=jax.ShapeDtypeStruct((k, points), jnp.bfloat16),
        grid=(points // width,),
        in_specs=[
            pl.BlockSpec(rows.shape, lambda i: (0, 0)),
            pl.BlockSpec((orb_val.shape[0], width), lambda i: (0, i)),
            pl.BlockSpec((orb_cond.shape[0], width), lambda i: (0, i)),
        ],
        out_specs=pl.BlockSpec((k, width), lambda i: (0, i)),
        name="encode",
    )(rows, orb_val, orb_cond)


def decode_kernel(val_ref, cond_ref, field_ref, out_ref):
    @pl.when(pl.program_id(0) == 0)
    def _():
        out_ref[...] = jnp.zeros_like(out_ref)

    field = field_ref[...]
    spread = jnp.concatenate(
        [field * cond_ref[c:c + 1, :] for c in range(cond_ref.shape[0])], axis=0
    )
    out_ref[...] += lax.dot_general(
        spread, val_ref[...], (((1,), (1,)), ((), ())), preferred_element_type=jnp.float32
    )


def decode(orb_val, orb_cond, field):
    k, points = field.shape
    width = math.gcd(points, 1024)
    rows = orb_cond.shape[0] * k
    return pl.pallas_call(
        decode_kernel,
        out_shape=jax.ShapeDtypeStruct((rows, orb_val.shape[0]), jnp.float32),
        grid=(points // width,),
        in_specs=[
            pl.BlockSpec((orb_val.shape[0], width), lambda i: (0, i)),
            pl.BlockSpec((orb_cond.shape[0], width), lambda i: (0, i)),
            pl.BlockSpec((k, width), lambda i: (0, i)),
        ],
        out_specs=pl.BlockSpec((rows, orb_val.shape[0]), lambda i: (0, 0)),
        name="decode",
    )(orb_val, orb_cond, field)


def staged_apply(rows, gap_rows, orb_val, orb_cond, kernel, k):
    part = encode(rows, orb_val, orb_cond, k)
    own = lax.psum_scatter(part, "val", scatter_dimension=1, tiled=True)
    fit = lax.psum(own, "pts")
    kernel_part = lax.dot_general(
        fit, kernel, (((1,), (1,)), ((), ())), preferred_element_type=jnp.float32
    )
    piece = lax.psum(kernel_part.astype(jnp.bfloat16), "val")
    field = lax.all_gather(piece, "pts", axis=1, tiled=True)
    coupled = decode(orb_val, orb_cond, field)
    current = rows.astype(jnp.float32)
    return (gap_rows * current + 2.0 * coupled - CENTER * current) / HALF_WIDTH


def on_device(A, B, trial, energy_gap, orb_val, orb_cond, kernel):
    k = trial.shape[1] // orb_cond.shape[0]
    rows = trial.T
    gap_rows = jnp.repeat(energy_gap.T, k, axis=0)
    Q = B // 2
    Z = math.gcd(Q, 4)
    Y = Q // Z
    points = orb_val.shape[1]
    w = points // (A * B)
    R = points // B
    if w % 128:
        first = staged_apply(rows, gap_rows, orb_val, orb_cond, kernel, k).astype(BF16)
        second = 2.0 * staged_apply(first, gap_rows, orb_val, orb_cond, kernel, k)
        return first.T, (second - rows.astype(F32)).astype(BF16).T
    sends = A + (A - 1) * 2 + (Y - 1) + (Z - 1) + 2 * (Z - 1 + (Y - 1) * Z + Q)
    vmem = pl.BlockSpec(memory_space=pltpu.VMEM)
    anywhere = pl.BlockSpec(memory_space=pl.ANY)
    cond_count = orb_cond.shape[0]
    kk = k // 2
    rows = trial.reshape(-1, cond_count, 2, kk).transpose(2, 1, 3, 0).reshape(rows.shape)
    gap_rows = jnp.repeat(energy_gap.T, kk, axis=0)
    shape = jax.ShapeDtypeStruct(rows.shape, BF16)
    first, second = pl.pallas_call(
        functools.partial(filter_kernel, (A, Y, Z)),
        out_shape=(shape, shape),
        in_specs=[vmem, vmem, vmem, anywhere, anywhere],
        out_specs=(vmem, vmem),
        scratch_shapes=[
            pltpu.VMEM(orb_val.shape, BF16),
            pltpu.VMEM(kernel.shape, BF16),
            pltpu.VMEM(rows.shape, BF16),
            pltpu.VMEM(rows.shape, F32),
            pltpu.VMEM((2, R, kk), F32),
            pltpu.VMEM((2, 2, A, Q, kk, w), BF16),
            pltpu.VMEM((2, 2, A, Q, kk, w), BF16),
            pltpu.VMEM((2, 2, A, Q, kk, w), BF16),
            pltpu.VMEM((2, 2, A, Q, kk, w), BF16),
            pltpu.VMEM((2, 2, max(A - 1, 1), Q, kk, w), BF16),
            pltpu.VMEM((2, 2, Y, Z, kk, w), BF16),
            pltpu.VMEM((2, 2, max(Y - 1, 1), Z, kk, w), BF16),
            pltpu.VMEM((2, 2, Z, kk, w), BF16),
            pltpu.VMEM((2, 2, max(Z - 1, 1), kk, w), BF16),
            pltpu.VMEM((2, 2, 2, Y, Z, kk, w), BF16),
            pltpu.VMEM((2, 2, kk, R), BF16),
            pltpu.VMEM((2, 2, max(A - 1, 1), kk, R), BF16),
            pltpu.VMEM((2, 2, 2, Y, Z, kk, R), BF16),
            pltpu.SemaphoreType.DMA((A * B,)),
            pltpu.SemaphoreType.DMA,
            pltpu.SemaphoreType.DMA((2, 2, sends)),
            pltpu.SemaphoreType.DMA((2, 2, sends)),
        ],
        compiler_params=pltpu.CompilerParams(
            collective_id=0, has_side_effects=True, vmem_limit_bytes=60 << 20),
        name="filter",
    )(rows, gap_rows, orb_cond, orb_val, kernel)

    def back(out):
        out = out.reshape(2, cond_count, kk, -1).transpose(3, 1, 0, 2)
        return out.reshape(trial.shape)

    return back(first), back(second)


def solution(mesh):
    placed = (P("val", "pts"), P("val", "pts"), P("val", None), P("pts", None), P("pts", "val"))
    return jax.shard_map(
        functools.partial(on_device, mesh.shape["val"], mesh.shape["pts"]),
        mesh=mesh,
        in_specs=placed,
        out_specs=(P("val", "pts"), P("val", "pts")),
        check_vma=False,
    )
```
